256 devices in a mesh: grp: 8 (over z_hi, core), dev: 32 (over y, x, z_lo).
Axes of the slice: x: 4, y: 4, z: 8 (z_hi: 4, z_lo: 2; z = z_hi * 2 + z_lo), core: 2. Of those that a mesh axis runs over, the one named last changes fastest.
Arguments:
- queries: float32 [256, 12, 128], P(('grp', 'dev')), may hold values from -2.1 to 2.1
- pages: float32 [256, 256, 128], P(('grp', 'dev')), may hold values from -2.1 to 2.1
- positive: int32 [256], replicated, may hold values from 0 to 255
Outputs:
- loss: float32 [], replicated
- question_token_slope: float32 [256, 12, 128], P(('grp', 'dev'))
- page_grad: float32 [256, 256, 128], P(('grp', 'dev'))
The draws below stay inside these ranges and needn't reach their ends.
All inputs are finite; a program needn't handle non-finite values.
Results may differ from the reference program's by a relative error of at most 0.00019.
Values sent between devices are 32-bit elements; how exact they have to be, the bound alone decides.
No kernel may reach another device: no remote copies, remote signals or barrier semaphores. Data moves between devices by JAX's collectives and lax.ppermute only.
A program may use at most 64 MiB of HBM per device.

```python
import jax
import jax.numpy as jnp
from jax import lax

W = 128
QTOK = 12
PAGE_TOK = 256
NQ = 256
NP = 256


def with_ends(result, own_key, least, largest):
    place = [jax.random.randint(jax.random.fold_in(own_key, axis), (), 0, length) for axis, length in enumerate(result.shape)]
    main_axis = result.shape.index(max(result.shape))
    neighbour = place[:main_axis] + [(place[main_axis] + 1) % result.shape[main_axis]] + place[main_axis + 1:]
    return result.at[tuple(place)].set(least).at[tuple(neighbour)].set(largest)


def steps_of(key, dims, cuts, least, largest):
    loudness = 1.0
    for dim, shards_of in cuts:
        draws = jax.random.uniform(jax.random.fold_in(jax.random.fold_in(key, 6), dim), (shards_of,), jnp.float32, least / len(cuts), largest / len(cuts))
        loudness = loudness * jnp.repeat(jnp.exp(draws), dims[dim] // shards_of).reshape((-1,) + (1,) * (len(dims) - 1 - dim))
    return loudness


def scatter_about(rng, extent, width, most, shards=(), held_as=jnp.bfloat16):
    values = jax.random.normal(rng, extent, jnp.float32) * width
    if len(shards) > 0:
        values = steps_of(rng, extent, shards, -0.22, 0.18) * values
    return jnp.clip(values, min=-most, max=most).astype(held_as)


def setup_inputs(seed: int = 0) -> dict:
    splits = jax.random.split(jax.random.key(seed), 4)
    queries = scatter_about(splits[0], (NQ, QTOK, W), 0.35, 2.1, ((0, 256),), jnp.float32)
    pages = scatter_about(splits[1], (NP, PAGE_TOK, W), 0.35, 2.1, ((0, 256),), jnp.float32)
    positive = with_ends(jax.random.randint(splits[2], (NQ,), 0, NP), jax.random.fold_in(splits[2], 1), 0, NP - 1).astype(jnp.int32)
    return dict(queries=queries, pages=pages, positive=positive)


cap_value = 4.0
sharpness_divisor = 0.25
logit_scale = 8.0
z_weight = 0.001
highest = lax.Precision.HIGHEST


def block_partial_terms(query_rows, page_rows, query_tokens):
    scores = jnp.dot(query_rows, page_rows.T, precision=highest, preferred_element_type=jnp.float32)
    tangent = jnp.tanh(scores / cap_value)
    bounded_similarity = cap_value * tangent
    exponential_grid = jnp.exp(bounded_similarity / sharpness_divisor)
    accumulated_totals = jnp.sum(exponential_grid, axis=1)
    gentle_peak = sharpness_divisor * jnp.log(accumulated_totals)
    slopes = exponential_grid / accumulated_totals[:, None] * (1.0 - tangent * tangent) * (logit_scale / query_tokens)
    return gentle_peak, slopes


def reference(queries, pages, positive):
    flattened_query_rows = queries.reshape(NQ * QTOK, W)

    def page_logits(page_rows):
        gentle_peak, unused_slopes = block_partial_terms(flattened_query_rows, page_rows, QTOK)
        return logit_scale / QTOK * gentle_peak.reshape(NQ, QTOK).sum(axis=1)

    logits = lax.map(page_logits, pages)
    exponential_grid = jnp.exp(logits)
    accumulated_totals = jnp.sum(exponential_grid, axis=0)
    log_totals = jnp.log(accumulated_totals)
    chosen = (positive[None, :] == jnp.arange(NP, dtype=jnp.int32)[:, None]).astype(jnp.float32)
    matching_logit = jnp.sum(chosen * logits, axis=0)
    loss = jnp.mean(log_totals - matching_logit + z_weight * log_totals * log_totals)
    coefficients = ((1.0 + 2.0 * z_weight * log_totals)[None, :] * exponential_grid / accumulated_totals[None, :] - chosen) / NQ

    def backward(query_total, inputs):
        page_rows, column = inputs
        unused_smooth, slopes = block_partial_terms(flattened_query_rows, page_rows, QTOK)
        token_grads = slopes * jnp.repeat(column, QTOK)[:, None]
        query_total = query_total + jnp.dot(token_grads, page_rows, precision=highest, preferred_element_type=jnp.float32)
        page_part = jnp.dot(token_grads.T, flattened_query_rows, precision=highest, preferred_element_type=jnp.float32)
        return query_total, page_part

    start_total = jnp.zeros((NQ * QTOK, W), jnp.float32)
    query_total, page_grad = lax.scan(backward, start_total, (pages, coefficients))
    return loss, query_total.reshape(NQ, QTOK, W), page_grad
```

```python
import itertools

import jax
import jax.numpy as jnp
from jax import lax
from jax.experimental import pallas as pl
from jax.experimental.pallas import tpu as pltpu
from jax.sharding import Mesh
from jax.sharding import PartitionSpec as P

AXES = ("za", "co", "y", "x", "zb")
SIZES = dict(za=4, co=2, y=4, x=4, zb=2)
QUERY_AXES = ("za", "y", "zb")
QN = 32
XN = 4
TOK = 12
ROWS = QN * TOK
PT = 256
W = 128
NQ = 256

cap_value = 4.0
sharpness_divisor = 0.25
logit_scale = 8.0
z_weight = 0.001
f32 = jnp.float32
bf16 = jnp.bfloat16


def iota(shape, dim):
    return lax.broadcasted_iota(jnp.int32, shape, dim)


def parts(x):
    high = x.astype(bf16)
    return high, (x - high.astype(f32)).astype(bf16)


def product(a, b, dims, a_axis, b_axis):
    left = jnp.concatenate([a[0], a[0], a[1]], axis=a_axis)
    right = jnp.concatenate([b[0], b[1], b[0]], axis=b_axis)
    return lax.dot_general(left, right, (dims, ((), ())), preferred_element_type=f32)


def spread_matrix():
    row, lane = iota((ROWS, 128), 0), iota((ROWS, 128), 1)
    first = (lane & 31) * TOK
    return ((row >= first) & (row < first + TOK) & (lane < 64)).astype(f32)


def page_terms(q_parts, pages, whi_ref, wlo_ref, ut_ref, tot_ref):
    for s, page_ref in enumerate(pages):
        page = page_ref[0]
        scores = product(parts(page), q_parts, ((1,), (0,)), 1, 0)
        tangent = jnp.tanh(scores * (1.0 / cap_value))
        grid = jnp.exp(tangent * (cap_value / sharpness_divisor))
        tot_ref[s : s + 1, :] = jnp.sum(grid, axis=0, keepdims=True)
        weights = parts(grid * (1.0 - tangent * tangent))
        whi_ref[s] = weights[0]
        wlo_ref[s] = weights[1]
        ut_ref[s] = product(parts(page.T), weights, ((1,), (0,)), 1, 0)


def own_side_kernel(q_ref, p0, p1, p2, p3, whi_ref, wlo_ref, ut_ref, tot_ref, qt_ref, rows_ref):
    for k in range(QN):
        rows_ref[k * TOK : (k + 1) * TOK, :] = q_ref[k]
    qt = rows_ref[...].T
    qt_ref[...] = qt
    page_terms(parts(qt), (p0, p1, p2, p3), whi_ref, wlo_ref, ut_ref, tot_ref)


def is_positive(me_ref, positive_ref):
    me = me_ref[0]
    base = me & 0b00100110
    index, lane = iota((NQ, 128), 0), iota((NQ, 128), 1)
    k = lane & 31
    query = ((k >> 3) << 6) + (((k >> 1) & 3) << 3) + (k & 1) + base
    chosen = jnp.dot(
        positive_ref[...].astype(f32), (index == query).astype(f32), precision=lax.Precision.HIGHEST,
        preferred_element_type=f32,
    )
    row = iota((8, 128), 0)
    x = (((me >> 1) & 3) - (row & 3)) & 3
    co = ((me >> 5) & 1) ^ (row >> 2)
    page = (me & 0b11011001) + (x << 1) + (co << 5)
    return page.astype(f32) == chosen


def other_side_kernel(
    me_ref, positive_ref, qt_ref, tot_a_ref, p0, p1, p2, p3,
    whi_ref, wlo_ref, ut_ref, tot_ref, logits_ref, stats_ref,
):
    page_terms(parts(qt_ref[...]), (p0, p1, p2, p3), whi_ref, wlo_ref, ut_ref, tot_ref.at[4:8])
    tot_ref[0:4, :] = tot_a_ref[...]
    smooth = sharpness_divisor * jnp.log(tot_ref[...])
    logits = (logit_scale / TOK) * jnp.dot(
        smooth, spread_matrix(), precision=lax.Precision.HIGHEST, preferred_element_type=f32
    )
    logits_ref[...] = logits
    lane = iota((8, 128), 1)
    matched = jnp.where(is_positive(me_ref, positive_ref), logits, 0.0)
    local = jnp.where(lane < 32, jnp.exp(logits), jnp.where(lane < 64, matched, 0.0))
    summed = jnp.sum(local, axis=0, keepdims=True)
    stats_ref[...] = jnp.broadcast_to(summed[None], stats_ref.shape)


def page_gradients(whi_ref, wlo_ref, qt, factors, out_ref):
    for s in range(XN):
        scaled = parts(qt * factors[s : s + 1, :])
        out_ref[s * PT : (s + 1) * PT, :] = product(
            (whi_ref[s], wlo_ref[s]), scaled, ((1,), (1,)), 1, 1
        )


def coefficient_kernel(
    me_ref, positive_ref, stats_ref, logits_ref, tot_ref, qt_ref, whi_ref, wlo_ref,
    out_ref, factors_ref,
):
    stats = jnp.sum(stats_ref[...], axis=0)
    lane = iota((1, 128), 1)
    totals = jnp.where(lane < 32, stats, 1.0)
    log_totals = jnp.log(totals)
    terms = jnp.where(
        lane < 32, log_totals + z_weight * log_totals * log_totals, jnp.where(lane < 64, -stats, 0.0)
    )
    loss = jnp.sum(terms, axis=1, keepdims=True) * (1.0 / NQ)
    out_ref[XN * PT :, :] = jnp.broadcast_to(loss, (8, 128))
    chosen = is_positive(me_ref, positive_ref).astype(f32)
    exponential = jnp.where(iota((8, 128), 1) < 32, jnp.exp(logits_ref[...]), 0.0)
    coefficients = (
        (1.0 + 2.0 * z_weight * log_totals) * exponential / totals - chosen
    ) * (1.0 / NQ)
    coefficients = jnp.where(iota((8, 128), 1) < 32, coefficients, 0.0)
    rows = lax.dot_general(
        coefficients, spread_matrix(), (((1,), (1,)), ((), ())), precision=lax.Precision.HIGHEST,
        preferred_element_type=f32,
    )
    factors = rows * (logit_scale / TOK) / tot_ref[...]
    factors_ref[...] = factors
    page_gradients(whi_ref, wlo_ref, qt_ref[...], factors[4:8], out_ref)


def gradient_kernel(factors_ref, qt_ref, whi_ref, wlo_ref, ut_a_ref, ut_b_ref, out_ref, dq_ref, rows_ref):
    factors = factors_ref[...]
    page_gradients(whi_ref, wlo_ref, qt_ref[...], factors[0:4], out_ref)
    total = jnp.zeros((W, ROWS), f32)
    for s in range(XN):
        total = total + ut_a_ref[s] * factors[s : s + 1, :]
        total = total + ut_b_ref[s] * factors[4 + s : 5 + s, :]
    rows_ref[...] = total.T
    for k in range(QN):
        dq_ref[k] = rows_ref[k * TOK : (k + 1) * TOK, :]


def pair_kernel(mine_ref, loss_ref, theirs_ref, o0, o1, o2, o3):
    loss = loss_ref[...] + theirs_ref[XN * PT :, :]
    for s, out in enumerate((o0, o1, o2, o3)):
        rows = slice(s * PT, (s + 1) * PT)
        out[0:PT, :] = mine_ref[rows, :] + theirs_ref[rows, :]
        out[PT:, :] = loss


def final_kernel(r0, r1, r2, r3, dq_ref, page_ref, loss_ref, slope_ref):
    total = (r0[...] + r2[...]) + (r1[...] + r3[...])
    page_ref[0] = total[0:PT]
    loss_ref[...] = total[PT:]
    slope_ref[0] = jnp.sum(dq_ref[...], axis=0)


def call(kernel, out, scratch=(), scalars=0):
    vmem = pl.BlockSpec(memory_space=pltpu.VMEM)

    def run(*args):
        specs = [pl.BlockSpec(memory_space=pltpu.SMEM)] * scalars + [vmem] * (len(args) - scalars)
        return pl.pallas_call(
            kernel,
            out_shape=[jax.ShapeDtypeStruct(s, d) for s, d in out],
            in_specs=specs,
            out_specs=[vmem] * len(out),
            scratch_shapes=list(scratch),
            compiler_params=pltpu.CompilerParams(vmem_limit_bytes=48 * 1024 * 1024),
        )(*args)

    return run


def moved(value, axis, step):
    n = SIZES[axis]
    return lax.ppermute(value, axis, [(i, (i + step) % n) for i in range(n)])


def shards(queries, pages, positive):
    me = lax.axis_index(AXES).astype(jnp.int32).reshape(1)
    positive = positive.reshape(1, NQ)
    own = [pages] + [moved(pages, "x", s) for s in range(1, XN)]
    spread = jnp.broadcast_to(queries, (QN, TOK, W))
    block = lax.all_to_all(spread, QUERY_AXES, 0, 0, tiled=True)
    other = [moved(page, "co", 1) for page in own]

    halves = [((XN, PT, ROWS), bf16), ((XN, PT, ROWS), bf16), ((XN, W, ROWS), f32)]
    whi_a, wlo_a, ut_a, tot_a, qt = call(
        own_side_kernel, halves + [((XN, ROWS), f32), ((W, ROWS), f32)],
        [pltpu.VMEM((ROWS, W), f32)],
    )(block, *own)
    whi_b, wlo_b, ut_b, tot, logits, stats = call(
        other_side_kernel,
        halves + [((2 * XN, ROWS), f32), ((8, 128), f32), ((QN, 1, 128), f32)],
        scalars=1,
    )(me, positive, qt, tot_a, *other)
    stats = lax.all_to_all(stats, QUERY_AXES, 0, 0, tiled=True)
    theirs, factors = call(
        coefficient_kernel, [((XN * PT + 8, W), f32), ((2 * XN, ROWS), f32)], scalars=1
    )(me, positive, stats, logits, tot, qt, whi_b, wlo_b)
    loss_rows = theirs[XN * PT :]
    theirs = moved(theirs, "co", 1)
    mine, dq = call(
        gradient_kernel, [((XN * PT, W), f32), ((QN, TOK, W), f32)], [pltpu.VMEM((ROWS, W), f32)]
    )(factors, qt, whi_a, wlo_a, ut_a, ut_b)
    sums = call(pair_kernel, [((PT + 8, W), f32)] * XN)(mine, loss_rows, theirs)
    sums = [sums[0]] + [moved(sums[s], "x", -s) for s in range(1, XN)]
    dq = lax.all_to_all(dq, QUERY_AXES, 0, 0, tiled=True)
    page_grad, loss, slope = call(
        final_kernel, [((1, PT, W), f32), ((8, 128), f32), ((1, TOK, W), f32)]
    )(*sums, dq)
    return loss[0, 0], slope, page_grad


def solution(mesh):
    finer = Mesh(mesh.devices.reshape(tuple(SIZES[a] for a in AXES)), AXES)
    placed = (P(AXES, None, None), P(AXES, None, None), P())
    return jax.shard_map(
        shards,
        mesh=finer,
        in_specs=placed,
        out_specs=(P(), P(AXES, None, None), P(AXES, None, None)),
        check_vma=False,
    )
```

```python
import itertools

import jax
import jax.numpy as jnp
from jax import lax
from jax.experimental import pallas as pl
from jax.experimental.pallas import tpu as pltpu
from jax.sharding import Mesh
from jax.sharding import PartitionSpec as P

AXES = ("za", "co", "y", "x", "zb")
SIZES = dict(za=4, co=2, y=4, x=4, zb=2)
QUERY_AXES = ("za", "y", "zb")
QN = 32
XN = 4
TOK = 12
ROWS = QN * TOK
PT = 256
W = 128
NQ = 256

cap_value = 4.0
sharpness_divisor = 0.25
logit_scale = 8.0
z_weight = 0.001
PREPARE_FLOPS = 5_000_000_000
f32 = jnp.float32
bf16 = jnp.bfloat16


def iota(shape, dim):
    return lax.broadcasted_iota(jnp.int32, shape, dim)


def parts(x):
    high = x.astype(bf16)
    return high, (x - high.astype(f32)).astype(bf16)


def product(a, b, dims, a_axis, b_axis):
    left = jnp.concatenate([a[0], a[0], a[1]], axis=a_axis)
    right = jnp.concatenate([b[0], b[1], b[0]], axis=b_axis)
    return lax.dot_general(left, right, (dims, ((), ())), preferred_element_type=f32)


def spread_matrix():
    row, lane = iota((ROWS, 128), 0), iota((ROWS, 128), 1)
    first = (lane & 31) * TOK
    return ((row >= first) & (row < first + TOK) & (lane < 64)).astype(f32)


def prepare_kernel(p0, p1, p2, p3, hi_ref, lo_ref):
    for s, page_ref in enumerate((p0, p1, p2, p3)):
        hi_ref[s], lo_ref[s] = parts(page_ref[0])


def spread_kernel(q_ref, out_ref, rows_ref):
    for i in range(TOK):
        rows_ref[i : i + 1, :] = q_ref[i]
    out_ref[...] = jnp.broadcast_to(rows_ref[...][None], (QN, TOK, W))


def is_positive(me_ref, positive_ref):
    me = me_ref[0]
    base = me & 0b00100110
    index, lane = iota((NQ, 128), 0), iota((NQ, 128), 1)
    k = lane & 31
    query = ((k >> 3) << 6) + (((k >> 1) & 3) << 3) + (k & 1) + base
    chosen = jnp.dot(
        positive_ref[...].astype(f32), (index == query).astype(f32), precision=lax.Precision.HIGHEST,
        preferred_element_type=f32,
    )
    row = iota((8, 128), 0)
    x = (((me >> 1) & 3) - (row & 3)) & 3
    co = ((me >> 5) & 1) ^ (row >> 2)
    page = (me & 0b11011001) + (x << 1) + (co << 5)
    return page.astype(f32) == chosen


def chosen_kernel(me_ref, positive_ref, chosen_ref):
    chosen_ref[...] = is_positive(me_ref, positive_ref).astype(f32)


def score_kernel(
    q_ref, chosen_ref, hi_a, lo_a, hi_b, lo_b,
    whi_ref, wlo_ref, tot_ref, qt_ref, logits_ref, stats_ref, rows_ref,
):
    for k in range(QN):
        rows_ref[k * TOK : (k + 1) * TOK, :] = q_ref[k]
    qt = rows_ref[...].T
    qt_ref[...] = qt
    q_parts = parts(qt)
    for s in range(2 * XN):
        hi, lo = (hi_a, lo_a) if s < XN else (hi_b, lo_b)
        scores = product((hi[s % XN], lo[s % XN]), q_parts, ((1,), (0,)), 1, 0)
        tangent = jnp.tanh(scores * (1.0 / cap_value))
        grid = jnp.exp(tangent * (cap_value / sharpness_divisor))
        tot_ref[s : s + 1, :] = jnp.sum(grid, axis=0, keepdims=True)
        whi_ref[s], wlo_ref[s] = parts(grid * (1.0 - tangent * tangent))
    smooth = sharpness_divisor * jnp.log(tot_ref[...])
    logits = (logit_scale / TOK) * jnp.dot(
        smooth, spread_matrix(), precision=lax.Precision.HIGHEST, preferred_element_type=f32
    )
    logits_ref[...] = logits
    lane = iota((8, 128), 1)
    matched = jnp.where(chosen_ref[...] > 0.5, logits, 0.0)
    local = jnp.where(lane < 32, jnp.exp(logits), jnp.where(lane < 64, matched, 0.0))
    summed = jnp.sum(local, axis=0, keepdims=True)
    stats_ref[...] = jnp.broadcast_to(summed[None], stats_ref.shape)


def by_row(values):
    return lax.dot_general(
        jnp.where(iota((8, 128), 1) < 32, values, 0.0), spread_matrix(), (((1,), (1,)), ((), ())),
        precision=lax.Precision.HIGHEST, preferred_element_type=f32,
    )


def query_sums_kernel(
    logits_ref, chosen_ref, tot_ref, whi_ref, wlo_ref, hi_a, lo_a, hi_b, lo_b, out_ref, rows_ref
):
    scale = (logit_scale / TOK) / tot_ref[...]
    weighted = by_row(jnp.exp(logits_ref[...])) * scale
    matched = by_row(chosen_ref[...]) * scale
    totals = [jnp.zeros((W, ROWS), f32)] * 2
    for s in range(2 * XN):
        hi, lo = (hi_a, lo_a) if s < XN else (hi_b, lo_b)
        turned = [half[s % XN].astype(f32).T.astype(bf16) for half in (hi, lo)]
        terms = product(turned, (whi_ref[s], wlo_ref[s]), ((1,), (0,)), 1, 0)
        totals = [t + terms * f[s : s + 1, :] for t, f in zip(totals, (weighted, matched))]
    for start, total in zip((0, TOK), totals):
        rows_ref[...] = total.T
        for k in range(QN):
            out_ref[k, start : start + TOK, :] = rows_ref[k * TOK : (k + 1) * TOK, :]


def page_gradients(whi_ref, wlo_ref, qt, factors, first, out_ref):
    for s in range(XN):
        scaled = parts(qt * factors[first + s : first + s + 1, :])
        out_ref[s * PT : (s + 1) * PT, :] = product(
            (whi_ref[first + s], wlo_ref[first + s]), scaled, ((1,), (1,)), 1, 1
        )


def coefficient_kernel(
    stats_ref, logits_ref, chosen_ref, tot_ref, qt_ref, whi_ref, wlo_ref,
    out_ref, factors_ref, owner_ref,
):
    stats = jnp.sum(stats_ref[...], axis=0)
    lane = iota((1, 128), 1)
    totals = jnp.where(lane < 32, stats, 1.0)
    log_totals = jnp.log(totals)
    terms = jnp.where(
        lane < 32, log_totals + z_weight * log_totals * log_totals, jnp.where(lane < 64, -stats, 0.0)
    )
    loss = jnp.sum(terms, axis=1, keepdims=True) * (1.0 / NQ)
    out_ref[XN * PT :, :] = jnp.broadcast_to(loss, (8, 128))
    slope = 1.0 + 2.0 * z_weight * log_totals
    owner_ref[...] = slope / totals * (1.0 / NQ)
    coefficients = (slope * jnp.exp(logits_ref[...]) / totals - chosen_ref[...]) * (1.0 / NQ)
    factors = by_row(coefficients) * (logit_scale / TOK) / tot_ref[...]
    factors_ref[...] = factors
    page_gradients(whi_ref, wlo_ref, qt_ref[...], factors, XN, out_ref)


def own_gradient_kernel(factors_ref, qt_ref, whi_ref, wlo_ref, out_ref):
    page_gradients(whi_ref, wlo_ref, qt_ref[...], factors_ref[...], 0, out_ref)


def pair_kernel(mine_ref, loss_ref, theirs_ref, o0, o1, o2, o3):
    loss = loss_ref[...] + theirs_ref[XN * PT :, :]
    for s, out in enumerate((o0, o1, o2, o3)):
        rows = slice(s * PT, (s + 1) * PT)
        out[0:PT, :] = mine_ref[rows, :] + theirs_ref[rows, :]
        out[PT:, :] = loss


def final_kernel(me_ref, owner_ref, r0, r1, r2, r3, sums_ref, page_ref, loss_ref, slope_ref):
    total = (r0[...] + r2[...]) + (r1[...] + r3[...])
    page_ref[0] = total[0:PT]
    loss_ref[...] = total[PT : PT + 1, 0:1]
    me = me_ref[0]
    k = ((me >> 6) << 3) + (((me >> 3) & 3) << 1) + (me & 1)
    mine = jnp.where(iota((1, 128), 1) == k, owner_ref[...], 0.0)
    weight = jnp.sum(mine, axis=1, keepdims=True)
    sums = jnp.sum(sums_ref[...], axis=0)
    slope = sums[0:TOK] * weight - sums[TOK:] * (1.0 / NQ)
    for i in range(TOK):
        slope_ref[i] = slope[i : i + 1, :]


def call(kernel, out, scratch=(), scalars=0, flops=None):
    vmem = pl.BlockSpec(memory_space=pltpu.VMEM)

    def run(*args):
        specs = [pl.BlockSpec(memory_space=pltpu.SMEM)] * scalars + [vmem] * (len(args) - scalars)
        return pl.pallas_call(
            kernel,
            out_shape=[jax.ShapeDtypeStruct(s, d) for s, d in out],
            in_specs=specs,
            out_specs=[vmem] * len(out),
            scratch_shapes=list(scratch),
            compiler_params=pltpu.CompilerParams(vmem_limit_bytes=16 * 1024 * 1024),
            cost_estimate=flops and pl.CostEstimate(flops=flops, transcendentals=0, bytes_accessed=0),
        )(*args)

    return run


def moved(value, axis, step):
    n = SIZES[axis]
    return lax.ppermute(value, axis, [(i, (i + step) % n) for i in range(n)])


def shards(queries, pages, positive):
    me = lax.axis_index(AXES).astype(jnp.int32).reshape(1)
    positive = positive.reshape(1, NQ)
    own = [pages] + [moved(pages, "x", s) for s in range(1, XN)]
    other = [moved(page, "co", 1) for page in own]
    (spread,) = call(spread_kernel, [((QN, TOK, W), f32)], [pltpu.VMEM((TOK, W), f32)])(
        queries.transpose(1, 0, 2)
    )
    block = lax.all_to_all(spread, QUERY_AXES, 0, 0, tiled=True)

    prepare = call(prepare_kernel, [((XN, PT, W), bf16)] * 2, flops=PREPARE_FLOPS)
    hi_a, lo_a = prepare(*own)
    hi_b, lo_b = prepare(*other)
    (chosen,) = call(chosen_kernel, [((8, 128), f32)], scalars=1)(me, positive)
    weights = ((2 * XN, PT, ROWS), bf16)
    whi, wlo, tot, qt, logits, stats = call(
        score_kernel,
        [weights, weights, ((2 * XN, ROWS), f32), ((W, ROWS), f32), ((8, 128), f32), ((QN, 1, 128), f32)],
        [pltpu.VMEM((ROWS, W), f32)],
    )(block, chosen, hi_a, lo_a, hi_b, lo_b)
    stats = lax.all_to_all(stats, QUERY_AXES, 0, 0, tiled=True)
    (sums,) = call(query_sums_kernel, [((QN, 2 * TOK, W), f32)], [pltpu.VMEM((ROWS, W), f32)])(
        logits, chosen, tot, whi, wlo, hi_a, lo_a, hi_b, lo_b
    )
    sums = lax.all_to_all(sums, QUERY_AXES, 0, 0, tiled=True)
    theirs, factors, owner = call(
        coefficient_kernel, [((XN * PT + 8, W), f32), ((2 * XN, ROWS), f32), ((1, 128), f32)]
    )(stats, logits, chosen, tot, qt, whi, wlo)
    loss_rows = theirs[XN * PT :]
    theirs = moved(theirs, "co", 1)
    (mine,) = call(own_gradient_kernel, [((XN * PT, W), f32)])(factors, qt, whi, wlo)
    blocks = call(pair_kernel, [((PT + 8, W), f32)] * XN)(mine, loss_rows, theirs)
    blocks = [blocks[0]] + [moved(blocks[s], "x", -s) for s in range(1, XN)]
    page_grad, loss, slope = call(
        final_kernel, [((1, PT, W), f32), ((1, 1), f32), ((TOK, 1, W), f32)], scalars=1
    )(me, owner, *blocks, sums)
    return loss.reshape(()), slope.transpose(1, 0, 2), page_grad


def solution(mesh):
    finer = Mesh(mesh.devices.reshape(tuple(SIZES[a] for a in AXES)), AXES)
    placed = (P(AXES, None, None), P(AXES, None, None), P())
    return jax.shard_map(
        shards,
        mesh=finer,
        in_specs=placed,
        out_specs=(P(), P(AXES, None, None), P(AXES, None, None)),
        check_vma=False,
    )
```

```python
import itertools

import jax
import jax.numpy as jnp
from jax import lax
from jax.experimental import pallas as pl
from jax.experimental.pallas import tpu as pltpu
from jax.sharding import Mesh
from jax.sharding import PartitionSpec as P

AXES = ("za", "co", "y", "x", "zb")
SIZES = dict(za=4, co=2, y=4, x=4, zb=2)
QUERY_AXES = ("za", "y", "zb")
QN = 32
XN = 4
TOK = 12
ROWS = QN * TOK
PT = 256
W = 128
NQ = 256

cap_value = 4.0
sharpness_divisor = 0.25
logit_scale = 8.0
z_weight = 0.001
PIECE = 2 * TOK + 1
f32 = jnp.float32
bf16 = jnp.bfloat16


def iota(shape, dim):
    return lax.broadcasted_iota(jnp.int32, shape, dim)


def parts(x):
    high = x.astype(bf16)
    return high, (x - high.astype(f32)).astype(bf16)


def product(a, b, dims, a_axis, b_axis):
    left = jnp.concatenate([a[0], a[0], a[1]], axis=a_axis)
    right = jnp.concatenate([b[0], b[1], b[0]], axis=b_axis)
    return lax.dot_general(left, right, (dims, ((), ())), preferred_element_type=f32)


def spread_matrix():
    row, lane = iota((ROWS, 128), 0), iota((ROWS, 128), 1)
    first = (lane & 31) * TOK
    return ((row >= first) & (row < first + TOK) & (lane < 64)).astype(f32)


def is_positive(me_ref, positive_ref):
    me = me_ref[0]
    base = me & 0b00100110
    index, lane = iota((NQ, 128), 0), iota((NQ, 128), 1)
    k = lane & 31
    query = ((k >> 3) << 6) + (((k >> 1) & 3) << 3) + (k & 1) + base
    chosen = jnp.dot(
        positive_ref[...].astype(f32), (index == query).astype(f32), precision=lax.Precision.HIGHEST,
        preferred_element_type=f32,
    )
    row = iota((8, 128), 0)
    x = (((me >> 1) & 3) - (row & 3)) & 3
    co = ((me >> 5) & 1) ^ (row >> 2)
    page = (me & 0b11011001) + (x << 1) + (co << 5)
    return page.astype(f32) == chosen


def by_row(values):
    return lax.dot_general(
        jnp.where(iota((8, 128), 1) < 32, values, 0.0), spread_matrix(), (((1,), (1,)), ((), ())),
        precision=lax.Precision.HIGHEST, preferred_element_type=f32,
    )


def score_kernel(
    me_ref, own_hbm, positive_hbm, q_ref, p1, p2, p3, p4, p5, p6, p7,
    whi_ref, wlo_ref, qt_ref, logits_ref, scale_ref, chosen_ref, sums_ref,
    tot_ref, rows_ref, p0, positive_ref, own_sem, positive_sem,
):
    own_copy = pltpu.make_async_copy(own_hbm, p0, own_sem)
    positive_copy = pltpu.make_async_copy(positive_hbm, positive_ref, positive_sem)
    own_copy.start()
    positive_copy.start()
    qt = q_ref[...].T
    qt_ref[...] = qt
    q_parts = parts(qt)
    pages = (p0, p1, p2, p3, p4, p5, p6, p7)
    for s, page_ref in [*enumerate(pages)][1:] + [(0, p0)]:
        if s == 0:
            own_copy.wait()
        scores = product(parts(page_ref[0]), q_parts, ((1,), (0,)), 1, 0)
        tangent = jnp.tanh(scores * (1.0 / cap_value))
        grid = jnp.exp(tangent * (cap_value / sharpness_divisor))
        tot_ref[s : s + 1, :] = jnp.sum(grid, axis=0, keepdims=True)
        whi_ref[s], wlo_ref[s] = parts(grid * (1.0 - tangent * tangent))
    smooth = sharpness_divisor * jnp.log(tot_ref[...])
    logits = (logit_scale / TOK) * jnp.dot(
        smooth, spread_matrix(), precision=lax.Precision.HIGHEST, preferred_element_type=f32
    )
    logits_ref[...] = logits
    positive_copy.wait()
    chosen = is_positive(me_ref, positive_ref)
    chosen_ref[...] = chosen.astype(f32)
    scale = (logit_scale / TOK) / tot_ref[...]
    scale_ref[...] = scale
    lane = iota((8, 128), 1)
    exponential = jnp.exp(logits)
    matched = jnp.where(chosen, logits, 0.0)
    local = jnp.where(lane < 32, exponential, jnp.where(lane < 64, matched, 0.0))
    stats = jnp.sum(local, axis=0, keepdims=True)

    weighted = by_row(exponential) * scale
    matched = by_row(chosen.astype(f32)) * scale
    totals = [jnp.zeros((W, ROWS), f32)] * 2
    for s, page_ref in enumerate(pages):
        terms = product(parts(page_ref[0].T), (whi_ref[s], wlo_ref[s]), ((1,), (0,)), 1, 0)
        totals = [t + terms * f[s : s + 1, :] for t, f in zip(totals, (weighted, matched))]
    for start, total in zip((0, TOK), totals):
        rows_ref[...] = total.T
        for k in range(QN):
            first = k * PIECE + start
            sums_ref[first : first + TOK, :] = rows_ref[k * TOK : (k + 1) * TOK, :]
    for k in range(QN):
        sums_ref[k * PIECE + 2 * TOK : (k + 1) * PIECE, :] = stats


def page_gradients(whi_ref, wlo_ref, qt, factors, first, out_ref):
    for s in range(XN):
        scaled = parts(qt * factors[first + s : first + s + 1, :])
        out_ref[s * PT : (s + 1) * PT, :] = product(
            (whi_ref[first + s], wlo_ref[first + s]), scaled, ((1,), (1,)), 1, 1
        )


def coefficient_kernel(
    sums_ref, logits_ref, chosen_ref, scale_ref, qt_ref, whi_ref, wlo_ref,
    out_ref, factors_ref, owner_ref,
):
    stats = jnp.zeros((1, 128), f32)
    for k in range(QN):
        stats = stats + sums_ref[k * PIECE + 2 * TOK : (k + 1) * PIECE, :]
    lane = iota((1, 128), 1)
    totals = jnp.where(lane < 32, stats, 1.0)
    log_totals = jnp.log(totals)
    terms = jnp.where(
        lane < 32, log_totals + z_weight * log_totals * log_totals, jnp.where(lane < 64, -stats, 0.0)
    )
    loss = jnp.sum(terms, axis=1, keepdims=True) * (1.0 / NQ)
    out_ref[XN * PT :, :] = jnp.broadcast_to(loss, (8, 128))
    slope = 1.0 + 2.0 * z_weight * log_totals
    owner_ref[...] = slope / totals * (1.0 / NQ)
    coefficients = (slope * jnp.exp(logits_ref[...]) / totals - chosen_ref[...]) * (1.0 / NQ)
    factors = by_row(coefficients) * scale_ref[...]
    factors_ref[...] = factors
    page_gradients(whi_ref, wlo_ref, qt_ref[...], factors, XN, out_ref)


def own_gradient_kernel(factors_ref, qt_ref, whi_ref, wlo_ref, out_ref):
    page_gradients(whi_ref, wlo_ref, qt_ref[...], factors_ref[...], 0, out_ref)


def pair_kernel(mine_ref, loss_ref, theirs_ref, o0, o1, o2, o3):
    loss = loss_ref[...] + theirs_ref[XN * PT :, :]
    for s, out in enumerate((o0, o1, o2, o3)):
        rows = slice(s * PT, (s + 1) * PT)
        out[0:PT, :] = mine_ref[rows, :] + theirs_ref[rows, :]
        out[PT:, :] = loss


def final_kernel(me_ref, owner_ref, r0, r1, r2, r3, sums_ref, page_ref, loss_ref, slope_ref):
    total = (r0[...] + r2[...]) + (r1[...] + r3[...])
    page_ref[0] = total[0:PT]
    loss_ref[...] = total[PT : PT + 1, 0:1]
    me = me_ref[0]
    k = ((me >> 6) << 3) + (((me >> 3) & 3) << 1) + (me & 1)
    mine = jnp.where(iota((1, 128), 1) == k, owner_ref[...], 0.0)
    weight = jnp.sum(mine, axis=1, keepdims=True)
    sums = jnp.zeros((2 * TOK, W), f32)
    for k in range(QN):
        sums = sums + sums_ref[k * PIECE : k * PIECE + 2 * TOK, :]
    slope = sums[0:TOK] * weight - sums[TOK:] * (1.0 / NQ)
    for i in range(TOK):
        slope_ref[i] = slope[i : i + 1, :]


def call(kernel, out, scratch=(), scalars=0, anywhere=0):
    vmem = pl.BlockSpec(memory_space=pltpu.VMEM)

    def run(*args):
        specs = [pl.BlockSpec(memory_space=pltpu.SMEM)] * scalars
        specs += [pl.BlockSpec(memory_space=pltpu.HBM)] * anywhere
        specs += [vmem] * (len(args) - scalars - anywhere)
        return pl.pallas_call(
            kernel,
            out_shape=[jax.ShapeDtypeStruct(s, d) for s, d in out],
            in_specs=specs,
            out_specs=[vmem] * len(out),
            scratch_shapes=list(scratch),
            compiler_params=pltpu.CompilerParams(vmem_limit_bytes=16 * 1024 * 1024),
        )(*args)

    return run


def moved(value, axis, step):
    n = SIZES[axis]
    return lax.ppermute(value, axis, [(i, (i + step) % n) for i in range(n)])


def shards(queries, pages, positive):
    me = lax.axis_index(AXES).astype(jnp.int32).reshape(1)
    positive = positive.reshape(1, NQ)
    rows = lax.optimization_barrier(queries.transpose(1, 0, 2))
    spread = jnp.broadcast_to(rows, (QN, TOK, 1, W))
    block = lax.all_to_all(spread, QUERY_AXES, 0, 0, tiled=True).reshape(ROWS, W)
    own = [pages] + [moved(pages, "x", s) for s in range(1, XN)]
    other = [moved(page, "co", 1) for page in own]

    weights, block_scalars = ((2 * XN, PT, ROWS), bf16), ((8, 128), f32)
    whi, wlo, qt, logits, scale, chosen, sums = call(
        score_kernel,
        [weights, weights, ((W, ROWS), f32), block_scalars, ((2 * XN, ROWS), f32), block_scalars,
         ((QN * PIECE, W), f32)],
        [pltpu.VMEM((2 * XN, ROWS), f32), pltpu.VMEM((ROWS, W), f32), pltpu.VMEM((1, PT, W), f32),
         pltpu.VMEM((1, NQ), jnp.int32), pltpu.SemaphoreType.DMA, pltpu.SemaphoreType.DMA],
        scalars=1, anywhere=2,
    )(me, pages, positive, block, *own[1:], *other)
    sums = lax.all_to_all(sums.reshape(QN, PIECE, 1, W), QUERY_AXES, 0, 0, tiled=True)
    sums = sums.reshape(QN * PIECE, W)
    theirs, factors, owner = call(
        coefficient_kernel, [((XN * PT + 8, W), f32), ((2 * XN, ROWS), f32), ((1, 128), f32)]
    )(sums, logits, chosen, scale, qt, whi, wlo)
    loss_rows = theirs[XN * PT :]
    theirs = moved(theirs, "co", 1)
    (mine,) = call(own_gradient_kernel, [((XN * PT, W), f32)])(factors, qt, whi, wlo)
    blocks = call(pair_kernel, [((PT + 8, W), f32)] * XN)(mine, loss_rows, theirs)
    blocks = [blocks[0]] + [moved(blocks[s], "x", -s) for s in range(1, XN)]
    page_grad, loss, slope = call(
        final_kernel, [((1, PT, W), f32), ((1, 1), f32), ((TOK, 1, W), f32)], scalars=1
    )(me, owner, *blocks, sums)
    return loss.reshape(()), slope.transpose(1, 0, 2), page_grad


def solution(mesh):
    finer = Mesh(mesh.devices.reshape(tuple(SIZES[a] for a in AXES)), AXES)
    placed = (P(AXES, None, None), P(AXES, None, None), P())
    return jax.shard_map(
        shards,
        mesh=finer,
        in_specs=placed,
        out_specs=(P(), P(AXES, None, None), P(AXES, None, None)),
        check_vma=False,
    )
```

```python
import jax
import jax.numpy as jnp
from jax import lax
from jax.experimental import pallas as pl
from jax.experimental.pallas import tpu as pltpu
from jax.sharding import Mesh
from jax.sharding import PartitionSpec as P

DEVICES = 256
CO, X = (5, 1), (1, 3)
QN = 32
QUERY_TURN = 0
STATS_TURN = 16
XN = 4
TOK = 12
ROWS = QN * TOK
PT = 256
W = 128
NQ = 256

cap_value = 4.0
sharpness_divisor = 0.25
logit_scale = 8.0
z_weight = 0.001
f32 = jnp.float32
bf16 = jnp.bfloat16


def offset_of(member):
    return ((member >> 3) << 6) + (((member >> 1) & 3) << 3) + (member & 1)


def groups(turn):
    members = [offset_of((k - turn) % QN) for k in range(QN)]
    return [[(co << 5) + (x << 1) + m for m in members] for co in range(2) for x in range(XN)]


def exchange(value, turn):
    return lax.all_to_all(value, "d", 0, 0, axis_index_groups=groups(turn), tiled=True)


def iota(shape, dim):
    return lax.broadcasted_iota(jnp.int32, shape, dim)


def parts(x):
    high = x.astype(bf16)
    return high, (x - high.astype(f32)).astype(bf16)


def product(a, b, dims):
    terms = [
        lax.dot_general(left, right, (dims, ((), ())), preferred_element_type=f32)
        for left, right in ((a[0], b[0]), (a[0], b[1]), (a[1], b[0]))
    ]
    return terms[0] + (terms[1] + terms[2])


def spread_matrix():
    row, lane = iota((ROWS, 128), 0), iota((ROWS, 128), 1)
    first = (lane & 31) * TOK
    return ((row >= first) & (row < first + TOK) & (lane < 64)).astype(f32)


def spread_kernel(q_hbm, out_ref, query_ref, rows_ref, sem):
    copy = pltpu.make_async_copy(q_hbm, query_ref, sem)
    copy.start()
    copy.wait()
    for i in range(TOK):
        rows_ref[i : i + 1, :] = query_ref[i]
        rows_ref[TOK + i : TOK + i + 1, :] = query_ref[i]
    twice = rows_ref[...]
    for k in range(QN // 2):
        out_ref[2 * k * TOK : 2 * (k + 1) * TOK, :] = twice


def is_positive(me_ref, positive_ref):
    me = me_ref[0]
    base = me & 0b00100110
    index, lane = iota((NQ, 128), 0), iota((NQ, 128), 1)
    query = offset_of((lane - QUERY_TURN) & (QN - 1)) + base
    chosen = jnp.dot(
        positive_ref[...].astype(f32), (index == query).astype(f32), precision=lax.Precision.HIGHEST,
        preferred_element_type=f32,
    )
    row = iota((8, 128), 0)
    x = (((me >> 1) & 3) - (row & 3)) & 3
    co = ((me >> 5) & 1) ^ (row >> 2)
    page = (me & 0b11011001) + (x << 1) + (co << 5)
    return page.astype(f32) == chosen


def by_row(values):
    return lax.dot_general(
        jnp.where(iota((8, 128), 1) < 32, values, 0.0), spread_matrix(), (((1,), (1,)), ((), ())),
        precision=lax.Precision.HIGHEST, preferred_element_type=f32,
    )


def score_kernel(
    me_ref, own_hbm, positive_hbm, q_ref, p1, p2, p3, p4, p5, p6, p7,
    whi_ref, wlo_ref, qt_ref, logits_ref, scale_ref, chosen_ref, ut_ref, stats_ref,
    tot_ref, p0, positive_ref, own_sem, positive_sem,
):
    own_copy = pltpu.make_async_copy(own_hbm, p0, own_sem)
    positive_copy = pltpu.make_async_copy(positive_hbm, positive_ref, positive_sem)
    own_copy.start()
    positive_copy.start()
    qt = q_ref[...].T
    qt_ref[...] = qt
    q_parts = parts(qt)
    pages = (p0, p1, p2, p3, p4, p5, p6, p7)
    for s, page_ref in [*enumerate(pages)][1:] + [(0, p0)]:
        if s == 0:
            own_copy.wait()
        scores = product(parts(page_ref[0]), q_parts, ((1,), (0,)))
        tangent = jnp.tanh(scores * (1.0 / cap_value))
        grid = jnp.exp(tangent * (cap_value / sharpness_divisor))
        tot_ref[s : s + 1, :] = jnp.sum(grid, axis=0, keepdims=True)
        whi_ref[s], wlo_ref[s] = parts(grid * (1.0 - tangent * tangent))
    smooth = sharpness_divisor * jnp.log(tot_ref[...])
    logits = (logit_scale / TOK) * jnp.dot(
        smooth, spread_matrix(), precision=lax.Precision.HIGHEST, preferred_element_type=f32
    )
    logits_ref[...] = logits
    positive_copy.wait()
    chosen = is_positive(me_ref, positive_ref)
    chosen_ref[...] = chosen.astype(f32)
    scale = (logit_scale / TOK) / tot_ref[...]
    scale_ref[...] = scale
    lane = iota((8, 128), 1)
    exponential = jnp.exp(logits)
    matched = jnp.where(chosen, logits, 0.0)
    local = jnp.where(lane < 32, exponential, jnp.where(lane < 64, matched, 0.0))
    stats = jnp.sum(local, axis=0, keepdims=True)

    stats_ref[...] = jnp.broadcast_to(stats[None], stats_ref.shape)
    for s, page_ref in enumerate(pages):
        ut_ref[s] = product(parts(page_ref[0].T), (whi_ref[s], wlo_ref[s]), ((1,), (0,)))


def page_gradients(whi_ref, wlo_ref, qt, factors, first, out_ref):
    for s in range(XN):
        scaled = parts(qt * factors[first + s : first + s + 1, :])
        out_ref[s * PT : (s + 1) * PT, :] = product(
            (whi_ref[first + s], wlo_ref[first + s]), scaled, ((1,), (1,))
        )


def coefficient_kernel(
    stats_ref, logits_ref, chosen_ref, scale_ref, qt_ref, whi_ref, wlo_ref, out_ref, factors_ref
):
    stats = jnp.sum(stats_ref[...], axis=0)
    lane = iota((1, 128), 1)
    totals = jnp.where(lane < 32, stats, 1.0)
    log_totals = jnp.log(totals)
    terms = jnp.where(
        lane < 32, log_totals + z_weight * log_totals * log_totals, jnp.where(lane < 64, -stats, 0.0)
    )
    loss = jnp.sum(terms, axis=1, keepdims=True) * (1.0 / NQ)
    out_ref[XN * PT :, :] = jnp.broadcast_to(loss, (8, 128))
    slope = 1.0 + 2.0 * z_weight * log_totals
    coefficients = (slope * jnp.exp(logits_ref[...]) / totals - chosen_ref[...]) * (1.0 / NQ)
    factors = by_row(coefficients) * scale_ref[...]
    factors_ref[...] = factors
    page_gradients(whi_ref, wlo_ref, qt_ref[...], factors, XN, out_ref)


def own_gradient_kernel(factors_ref, qt_ref, whi_ref, wlo_ref, ut_ref, out_ref, dq_ref):
    factors = factors_ref[...]
    total = jnp.zeros((W, ROWS), f32)
    for s in range(2 * XN):
        total = total + ut_ref[s] * factors[s : s + 1, :]
    dq_ref[...] = total.T
    page_gradients(whi_ref, wlo_ref, qt_ref[...], factors, 0, out_ref)


def pair_kernel(mine_ref, loss_ref, theirs_ref, o0, o1, o2, o3):
    loss = loss_ref[...] + theirs_ref[XN * PT :, :]
    for s, out in enumerate((o0, o1, o2, o3)):
        rows = slice(s * PT, (s + 1) * PT)
        out[0:PT, :] = mine_ref[rows, :] + theirs_ref[rows, :]
        out[PT:, :] = loss


def final_kernel(r0, r1, r2, r3, dq_ref, page_ref, loss_ref, slope_ref):
    total = (r0[...] + r2[...]) + (r1[...] + r3[...])
    page_ref[0] = total[0:PT]
    loss_ref[...] = total[PT : PT + 1, 0:1]
    slope = jnp.zeros((TOK, W), f32)
    for k in range(QN):
        slope = slope + dq_ref[k * TOK : (k + 1) * TOK, :]
    for i in range(TOK):
        slope_ref[i] = slope[i : i + 1, :]


def call(kernel, out, scratch=(), scalars=0, anywhere=0):
    vmem = pl.BlockSpec(memory_space=pltpu.VMEM)

    def run(*args):
        args = [
            pltpu.with_memory_space_constraint(a, pltpu.HBM) if scalars <= i < scalars + anywhere else a
            for i, a in enumerate(args)
        ]
        specs = [pl.BlockSpec(memory_space=pltpu.SMEM)] * scalars
        specs += [pl.BlockSpec(memory_space=pltpu.HBM)] * anywhere
        specs += [vmem] * (len(args) - scalars - anywhere)
        return pl.pallas_call(
            kernel,
            out_shape=[jax.ShapeDtypeStruct(s, d) for s, d in out],
            in_specs=specs,
            out_specs=[vmem] * len(out),
            scratch_shapes=list(scratch),
            compiler_params=pltpu.CompilerParams(vmem_limit_bytes=16 * 1024 * 1024),
        )(*args)

    return run


def moved(value, axis, step):
    bit, mask = axis
    pairs = [
        (i, (i & ~(mask << bit)) | ((((i >> bit) + step) & mask) << bit)) for i in range(DEVICES)
    ]
    return lax.ppermute(value, "d", pairs)


def shards(queries, pages, positive):
    me = lax.axis_index("d").astype(jnp.int32).reshape(1)
    positive = positive.reshape(1, NQ)
    (spread,) = call(
        spread_kernel, [((ROWS, W), f32)],
        [pltpu.VMEM((TOK, 1, W), f32), pltpu.VMEM((2 * TOK, W), f32), pltpu.SemaphoreType.DMA],
        anywhere=1,
    )(queries.transpose(1, 0, 2))
    block = exchange(spread.reshape(QN, TOK, 1, W), QUERY_TURN).reshape(ROWS, W)
    own = [pages] + [moved(pages, X, s) for s in range(1, XN)]
    other = [moved(page, CO, 1) for page in own]

    weights, block_scalars = ((2 * XN, PT, ROWS), bf16), ((8, 128), f32)
    whi, wlo, qt, logits, scale, chosen, ut, stats = call(
        score_kernel,
        [weights, weights, ((W, ROWS), f32), block_scalars, ((2 * XN, ROWS), f32), block_scalars,
         ((2 * XN, W, ROWS), f32), ((QN, 1, W), f32)],
        [pltpu.VMEM((2 * XN, ROWS), f32), pltpu.VMEM((1, PT, W), f32),
         pltpu.VMEM((1, NQ), jnp.int32), pltpu.SemaphoreType.DMA, pltpu.SemaphoreType.DMA],
        scalars=1, anywhere=2,
    )(me, pages, positive, block, *own[1:], *other)
    stats = exchange(stats, STATS_TURN)
    theirs, factors = call(
        coefficient_kernel, [((XN * PT + 8, W), f32), ((2 * XN, ROWS), f32)]
    )(stats, logits, chosen, scale, qt, whi, wlo)
    loss_rows = theirs[XN * PT :]
    theirs = moved(theirs, CO, 1)
    mine, dq = call(own_gradient_kernel, [((XN * PT, W), f32), ((ROWS, W), f32)])(
        factors, qt, whi, wlo, ut
    )
    blocks = call(pair_kernel, [((PT + 8, W), f32)] * XN)(mine, loss_rows, theirs)
    blocks = [blocks[0]] + [moved(blocks[s], X, -s) for s in range(1, XN)]
    dq = exchange(dq.reshape(QN, TOK, 1, W), QUERY_TURN)
    page_grad, loss, slope = call(
        final_kernel, [((1, PT, W), f32), ((1, 1), f32), ((TOK, 1, W), f32)]
    )(*blocks, dq.reshape(ROWS, W))
    return loss.reshape(()), slope.transpose(1, 0, 2), page_grad


def solution(mesh):
    flat = Mesh(mesh.devices.reshape(DEVICES), ("d",))
    placed = (P("d", None, None), P("d", None, None), P())
    return jax.shard_map(
        shards,
        mesh=flat,
        in_specs=placed,
        out_specs=(P(), P("d", None, None), P("d", None, None)),
        check_vma=False,
    )
```

```python
import jax
import jax.numpy as jnp
from jax import lax
from jax.experimental import pallas as pl
from jax.experimental.pallas import tpu as pltpu
from jax.sharding import Mesh
from jax.sharding import PartitionSpec as P

DEVICES = 256
CO, X = (5, 1), (1, 3)
QN = 32
QUERY_TURN = 0
STATS_TURN = 16
XN = 4
TOK = 12
ROWS = QN * TOK
PT = 256
W = 128
NQ = 256

cap_value = 4.0
sharpness_divisor = 0.25
logit_scale = 8.0
z_weight = 0.001
f32 = jnp.float32
bf16 = jnp.bfloat16


def offset_of(member):
    return ((member >> 3) << 6) + (((member >> 1) & 3) << 3) + (member & 1)


def groups(turn):
    members = [offset_of((k - turn) % QN) for k in range(QN)]
    return [[(co << 5) + (x << 1) + m for m in members] for co in range(2) for x in range(XN)]


def exchange(value, turn):
    return lax.all_to_all(value, "d", 0, 0, axis_index_groups=groups(turn), tiled=True)


def iota(shape, dim):
    return lax.broadcasted_iota(jnp.int32, shape, dim)


def parts(x):
    high = x.astype(bf16)
    return high, (x - high.astype(f32)).astype(bf16)


def product(a, b, dims):
    terms = [
        lax.dot_general(left, right, (dims, ((), ())), preferred_element_type=f32)
        for left, right in ((a[0], b[0]), (a[0], b[1]), (a[1], b[0]))
    ]
    return terms[0] + (terms[1] + terms[2])


def spread_matrix():
    row, lane = iota((ROWS, 128), 0), iota((ROWS, 128), 1)
    first = (lane & 31) * TOK
    return ((row >= first) & (row < first + TOK) & (lane < 64)).astype(f32)


def spread_kernel(q_hbm, out_ref, query_ref, rows_ref, sem):
    copy = pltpu.make_async_copy(q_hbm, query_ref, sem)
    copy.start()
    copy.wait()
    for i in range(TOK):
        rows_ref[i : i + 1, :] = query_ref[i]
        rows_ref[TOK + i : TOK + i + 1, :] = query_ref[i]
    twice = rows_ref[...]
    for k in range(QN // 2):
        out_ref[2 * k * TOK : 2 * (k + 1) * TOK, :] = twice


def is_positive(me_ref, positive_ref):
    me = me_ref[0]
    base = me & 0b00100110
    index, lane = iota((NQ, 128), 0), iota((NQ, 128), 1)
    query = offset_of((lane - QUERY_TURN) & (QN - 1)) + base
    chosen = jnp.dot(
        positive_ref[...].astype(f32), (index == query).astype(f32), precision=lax.Precision.HIGHEST,
        preferred_element_type=f32,
    )
    row = iota((8, 128), 0)
    x = (((me >> 1) & 3) - (row & 3)) & 3
    co = ((me >> 5) & 1) ^ (row >> 2)
    page = (me & 0b11011001) + (x << 1) + (co << 5)
    return page.astype(f32) == chosen


def by_row(values):
    return lax.dot_general(
        jnp.where(iota((8, 128), 1) < 32, values, 0.0), spread_matrix(), (((1,), (1,)), ((), ())),
        precision=lax.Precision.HIGHEST, preferred_element_type=f32,
    )


def page_terms(q_parts, page, s, whi_ref, wlo_ref, tot_ref):
    scores = product(parts(page), q_parts, ((1,), (0,)))
    tangent = jnp.tanh(scores * (1.0 / cap_value))
    grid = jnp.exp(tangent * (cap_value / sharpness_divisor))
    tot_ref[s : s + 1, :] = jnp.sum(grid, axis=0, keepdims=True)
    whi_ref[s], wlo_ref[s] = parts(grid * (1.0 - tangent * tangent))


def query_terms(page, s, whi_ref, wlo_ref, ut_ref):
    ut_ref[s] = product(parts(page.T), (whi_ref[s], wlo_ref[s]), ((1,), (0,)))


def own_score_kernel(
    me_ref, own_hbm, positive_hbm, q_ref, p1, p2, p3,
    whi_ref, wlo_ref, ut_ref, tot_ref, qt_ref, chosen_ref, p0, positive_ref, own_sem, positive_sem,
):
    own_copy = pltpu.make_async_copy(own_hbm, p0, own_sem)
    positive_copy = pltpu.make_async_copy(positive_hbm, positive_ref, positive_sem)
    own_copy.start()
    positive_copy.start()
    qt = q_ref[...].T
    qt_ref[...] = qt
    q_parts = parts(qt)
    pages = (p0, p1, p2, p3)
    for s in range(1, XN):
        page_terms(q_parts, pages[s][0], s, whi_ref, wlo_ref, tot_ref)
    own_copy.wait()
    page_terms(q_parts, p0[0], 0, whi_ref, wlo_ref, tot_ref)
    for s in range(XN):
        query_terms(pages[s][0], s, whi_ref, wlo_ref, ut_ref)
    positive_copy.wait()
    chosen_ref[...] = is_positive(me_ref, positive_ref).astype(f32)


def score_kernel(
    qt_ref, tot_a_ref, chosen_ref, p0, p1, p2, p3,
    whi_ref, wlo_ref, ut_ref, logits_ref, scale_ref, stats_ref, tot_ref,
):
    tot_ref[0:XN, :] = tot_a_ref[...]
    q_parts = parts(qt_ref[...])
    pages = (p0, p1, p2, p3)
    for s in range(XN):
        page_terms(q_parts, pages[s][0], s, whi_ref, wlo_ref, tot_ref.at[XN : 2 * XN])
    smooth = sharpness_divisor * jnp.log(tot_ref[...])
    logits = (logit_scale / TOK) * jnp.dot(
        smooth, spread_matrix(), precision=lax.Precision.HIGHEST, preferred_element_type=f32
    )
    logits_ref[...] = logits
    scale_ref[...] = (logit_scale / TOK) / tot_ref[...]
    lane = iota((8, 128), 1)
    matched = jnp.where(chosen_ref[...] > 0.5, logits, 0.0)
    local = jnp.where(lane < 32, jnp.exp(logits), jnp.where(lane < 64, matched, 0.0))
    stats = jnp.sum(local, axis=0, keepdims=True)
    stats_ref[...] = jnp.broadcast_to(stats[None], stats_ref.shape)
    for s in range(XN):
        query_terms(pages[s][0], s, whi_ref, wlo_ref, ut_ref)


def page_gradients(whi_ref, wlo_ref, qt, factors, first, out_ref):
    for s in range(XN):
        scaled = parts(qt * factors[first + s : first + s + 1, :])
        out_ref[s * PT : (s + 1) * PT, :] = product(
            (whi_ref[s], wlo_ref[s]), scaled, ((1,), (1,))
        )


def coefficient_kernel(
    stats_ref, logits_ref, chosen_ref, scale_ref, qt_ref, whi_ref, wlo_ref, ut_a_ref, ut_b_ref,
    out_ref, factors_ref, dq_ref,
):
    stats = jnp.sum(stats_ref[...], axis=0)
    lane = iota((1, 128), 1)
    totals = jnp.where(lane < 32, stats, 1.0)
    log_totals = jnp.log(totals)
    terms = jnp.where(
        lane < 32, log_totals + z_weight * log_totals * log_totals, jnp.where(lane < 64, -stats, 0.0)
    )
    loss = jnp.sum(terms, axis=1, keepdims=True) * (1.0 / NQ)
    out_ref[XN * PT :, :] = jnp.broadcast_to(loss, (8, 128))
    slope = 1.0 + 2.0 * z_weight * log_totals
    coefficients = (slope * jnp.exp(logits_ref[...]) / totals - chosen_ref[...]) * (1.0 / NQ)
    factors = by_row(coefficients) * scale_ref[...]
    factors_ref[...] = factors
    total = jnp.zeros((W, ROWS), f32)
    for s in range(XN):
        total = total + ut_a_ref[s] * factors[s : s + 1, :]
        total = total + ut_b_ref[s] * factors[XN + s : XN + s + 1, :]
    dq_ref[...] = total.T
    page_gradients(whi_ref, wlo_ref, qt_ref[...], factors, XN, out_ref)


def own_gradient_kernel(factors_ref, qt_ref, whi_ref, wlo_ref, out_ref):
    page_gradients(whi_ref, wlo_ref, qt_ref[...], factors_ref[...], 0, out_ref)


def pair_kernel(mine_ref, loss_ref, theirs_ref, o0, o1, o2, o3):
    loss = loss_ref[...] + theirs_ref[XN * PT :, :]
    for s, out in enumerate((o0, o1, o2, o3)):
        rows = slice(s * PT, (s + 1) * PT)
        out[0:PT, :] = mine_ref[rows, :] + theirs_ref[rows, :]
        out[PT:, :] = loss


def final_kernel(r0, r1, r2, r3, dq_ref, page_ref, loss_ref, slope_ref):
    total = (r0[...] + r2[...]) + (r1[...] + r3[...])
    page_ref[0] = total[0:PT]
    loss_ref[...] = total[PT : PT + 1, 0:1]
    slope = jnp.zeros((TOK, W), f32)
    for k in range(QN):
        slope = slope + dq_ref[k * TOK : (k + 1) * TOK, :]
    for i in range(TOK):
        slope_ref[i] = slope[i : i + 1, :]


def call(kernel, out, scratch=(), scalars=0, anywhere=0):
    vmem = pl.BlockSpec(memory_space=pltpu.VMEM)

    def run(*args):
        args = [
            pltpu.with_memory_space_constraint(a, pltpu.HBM) if scalars <= i < scalars + anywhere else a
            for i, a in enumerate(args)
        ]
        specs = [pl.BlockSpec(memory_space=pltpu.SMEM)] * scalars
        specs += [pl.BlockSpec(memory_space=pltpu.HBM)] * anywhere
        specs += [vmem] * (len(args) - scalars - anywhere)
        return pl.pallas_call(
            kernel,
            out_shape=[jax.ShapeDtypeStruct(s, d) for s, d in out],
            in_specs=specs,
            out_specs=[vmem] * len(out),
            scratch_shapes=list(scratch),
            compiler_params=pltpu.CompilerParams(vmem_limit_bytes=16 * 1024 * 1024),
        )(*args)

    return run


def moved(value, axis, step):
    bit, mask = axis
    pairs = [
        (i, (i & ~(mask << bit)) | ((((i >> bit) + step) & mask) << bit)) for i in range(DEVICES)
    ]
    return lax.ppermute(value, "d", pairs)


def shards(queries, pages, positive):
    me = lax.axis_index("d").astype(jnp.int32).reshape(1)
    positive = positive.reshape(1, NQ)
    (spread,) = call(
        spread_kernel, [((ROWS, W), f32)],
        [pltpu.VMEM((TOK, 1, W), f32), pltpu.VMEM((2 * TOK, W), f32), pltpu.SemaphoreType.DMA],
        anywhere=1,
    )(queries.transpose(1, 0, 2))
    block = exchange(spread.reshape(QN, TOK, 1, W), QUERY_TURN).reshape(ROWS, W)
    own = [pages] + [moved(pages, X, s) for s in range(1, XN)]
    other = [moved(page, CO, 1) for page in own]

    weights, terms = ((XN, PT, ROWS), bf16), ((XN, W, ROWS), f32)
    whi_a, wlo_a, ut_a, tot_a, qt, chosen = call(
        own_score_kernel,
        [weights, weights, terms, ((XN, ROWS), f32), ((W, ROWS), f32), ((8, 128), f32)],
        [pltpu.VMEM((1, PT, W), f32), pltpu.VMEM((1, NQ), jnp.int32),
         pltpu.SemaphoreType.DMA, pltpu.SemaphoreType.DMA],
        scalars=1, anywhere=2,
    )(me, pages, positive, block, *own[1:])
    whi_b, wlo_b, ut_b, logits, scale, stats = call(
        score_kernel,
        [weights, weights, terms, ((8, 128), f32), ((2 * XN, ROWS), f32), ((QN, 1, W), f32)],
        [pltpu.VMEM((2 * XN, ROWS), f32)],
    )(qt, tot_a, chosen, *other)
    stats = exchange(stats, STATS_TURN)
    theirs, factors, dq = call(
        coefficient_kernel, [((XN * PT + 8, W), f32), ((2 * XN, ROWS), f32), ((ROWS, W), f32)]
    )(stats, logits, chosen, scale, qt, whi_b, wlo_b, ut_a, ut_b)
    loss_rows = theirs[XN * PT :]
    theirs = moved(theirs, CO, 1)
    (mine,) = call(own_gradient_kernel, [((XN * PT, W), f32)])(factors, qt, whi_a, wlo_a)
    blocks = call(pair_kernel, [((PT + 8, W), f32)] * XN)(mine, loss_rows, theirs)
    blocks = [blocks[0]] + [moved(blocks[s], X, -s) for s in range(1, XN)]
    dq = exchange(dq.reshape(QN, TOK, 1, W), QUERY_TURN)
    page_grad, loss, slope = call(
        final_kernel, [((1, PT, W), f32), ((1, 1), f32), ((TOK, 1, W), f32)]
    )(*blocks, dq.reshape(ROWS, W))
    return loss.reshape(()), slope.transpose(1, 0, 2), page_grad


def solution(mesh):
    flat = Mesh(mesh.devices.reshape(DEVICES), ("d",))
    placed = (P("d", None, None), P("d", None, None), P())
    return jax.shard_map(
        shards,
        mesh=flat,
        in_specs=placed,
        out_specs=(P(), P("d", None, None), P("d", None, None)),
        check_vma=False,
    )
```

```python
import jax
import jax.numpy as jnp
from jax import lax
from jax.experimental import pallas as pl
from jax.experimental.pallas import tpu as pltpu
from jax.sharding import Mesh
from jax.sharding import PartitionSpec as P

DEVICES = 256
CO, X = (5, 1), (1, 3)
QN = 32
QUERY_ORDER = (0, 1)
STATS_ORDER = (7, -1)
XN = 4
TOK = 12
ROWS = QN * TOK
PT = 256
W = 128
NQ = 256

cap_value = 4.0
sharpness_divisor = 0.25
logit_scale = 8.0
z_weight = 0.001
f32 = jnp.float32
bf16 = jnp.bfloat16


def offset_of(member):
    return ((member >> 3) << 6) + (((member >> 1) & 3) << 3) + (member & 1)


def groups(order):
    first, step = order
    members = [offset_of((first + step * k) % QN) for k in range(QN)]
    return [[(co << 5) + (x << 1) + m for m in members] for co in range(2) for x in range(XN)]


def exchange(value, order):
    return lax.all_to_all(value, "d", 0, 0, axis_index_groups=groups(order), tiled=True)


def iota(shape, dim):
    return lax.broadcasted_iota(jnp.int32, shape, dim)


def parts(x):
    high = x.astype(bf16)
    return high, (x - high.astype(f32)).astype(bf16)


def product(a, b, dims):
    terms = [
        lax.dot_general(left, right, (dims, ((), ())), preferred_element_type=f32)
        for left, right in ((a[0], b[0]), (a[0], b[1]), (a[1], b[0]))
    ]
    return terms[0] + (terms[1] + terms[2])


def spread_matrix():
    row, lane = iota((ROWS, 128), 0), iota((ROWS, 128), 1)
    first = (lane & 31) * TOK
    return ((row >= first) & (row < first + TOK) & (lane < 64)).astype(f32)


def spread_kernel(q_hbm, out_ref, query_ref, rows_ref, sem):
    copy = pltpu.make_async_copy(q_hbm, query_ref, sem)
    copy.start()
    copy.wait()
    for i in range(TOK):
        rows_ref[i : i + 1, :] = query_ref[i]
        rows_ref[TOK + i : TOK + i + 1, :] = query_ref[i]
    twice = rows_ref[...]
    for k in range(QN // 2):
        out_ref[2 * k * TOK : 2 * (k + 1) * TOK, :] = twice


def is_positive(me_ref, positive_ref):
    me = me_ref[0]
    base = me & 0b00100110
    index, lane = iota((NQ, 128), 0), iota((NQ, 128), 1)
    query = offset_of((QUERY_ORDER[0] + QUERY_ORDER[1] * lane) & (QN - 1)) + base
    chosen = jnp.dot(
        positive_ref[...].astype(f32), (index == query).astype(f32), precision=lax.Precision.HIGHEST,
        preferred_element_type=f32,
    )
    row = iota((8, 128), 0)
    x = (((me >> 1) & 3) - (row & 3)) & 3
    co = ((me >> 5) & 1) ^ (row >> 2)
    page = (me & 0b11011001) + (x << 1) + (co << 5)
    return page.astype(f32) == chosen


def by_row(values):
    return lax.dot_general(
        jnp.where(iota((8, 128), 1) < 32, values, 0.0), spread_matrix(), (((1,), (1,)), ((), ())),
        precision=lax.Precision.HIGHEST, preferred_element_type=f32,
    )


def page_terms(q_parts, page, s, whi_ref, wlo_ref, tot_ref):
    scores = product(parts(page), q_parts, ((1,), (0,)))
    tangent = jnp.tanh(scores * (1.0 / cap_value))
    grid = jnp.exp(tangent * (cap_value / sharpness_divisor))
    tot_ref[s : s + 1, :] = jnp.sum(grid, axis=0, keepdims=True)
    whi_ref[s], wlo_ref[s] = parts(grid * (1.0 - tangent * tangent))


def query_terms(page, s, whi_ref, wlo_ref, ut_ref):
    ut_ref[s] = product(parts(page.T), (whi_ref[s], wlo_ref[s]), ((1,), (0,)))


def own_score_kernel(
    me_ref, own_hbm, positive_hbm, q_ref, p1, p2, p3,
    whi_ref, wlo_ref, ut_ref, tot_ref, qt_ref, chosen_ref, p0, positive_ref, own_sem, positive_sem,
):
    own_copy = pltpu.make_async_copy(own_hbm, p0, own_sem)
    positive_copy = pltpu.make_async_copy(positive_hbm, positive_ref, positive_sem)
    own_copy.start()
    positive_copy.start()
    qt = q_ref[...].T
    qt_ref[...] = qt
    q_parts = parts(qt)
    pages = (p0, p1, p2, p3)
    for s in range(1, XN):
        page_terms(q_parts, pages[s][0], s, whi_ref, wlo_ref, tot_ref)
    own_copy.wait()
    page_terms(q_parts, p0[0], 0, whi_ref, wlo_ref, tot_ref)
    for s in range(XN):
        query_terms(pages[s][0], s, whi_ref, wlo_ref, ut_ref)
    positive_copy.wait()
    chosen_ref[...] = is_positive(me_ref, positive_ref).astype(f32)


def score_kernel(
    qt_ref, tot_a_ref, chosen_ref, p0, p1, p2, p3,
    whi_ref, wlo_ref, ut_ref, logits_ref, scale_ref, stats_ref, tot_ref,
):
    tot_ref[0:XN, :] = tot_a_ref[...]
    q_parts = parts(qt_ref[...])
    pages = (p0, p1, p2, p3)
    for s in range(XN):
        page_terms(q_parts, pages[s][0], s, whi_ref, wlo_ref, tot_ref.at[XN : 2 * XN])
    smooth = sharpness_divisor * jnp.log(tot_ref[...])
    logits = (logit_scale / TOK) * jnp.dot(
        smooth, spread_matrix(), precision=lax.Precision.HIGHEST, preferred_element_type=f32
    )
    logits_ref[...] = logits
    scale_ref[...] = (logit_scale / TOK) / tot_ref[...]
    lane = iota((8, 128), 1)
    matched = jnp.where(chosen_ref[...] > 0.5, logits, 0.0)
    local = jnp.where(lane < 32, jnp.exp(logits), jnp.where(lane < 64, matched, 0.0))
    stats = jnp.sum(local, axis=0, keepdims=True)
    stats_ref[...] = jnp.broadcast_to(stats[None], stats_ref.shape)
    for s in range(XN):
        query_terms(pages[s][0], s, whi_ref, wlo_ref, ut_ref)


def page_gradients(whi_ref, wlo_ref, qt, factors, first, out_ref):
    for s in range(XN):
        scaled = parts(qt * factors[first + s : first + s + 1, :])
        out_ref[s * PT : (s + 1) * PT, :] = product(
            (whi_ref[s], wlo_ref[s]), scaled, ((1,), (1,))
        )


def coefficient_kernel(
    stats_ref, logits_ref, chosen_ref, scale_ref, qt_ref, whi_ref, wlo_ref, ut_a_ref, ut_b_ref,
    out_ref, factors_ref, dq_ref,
):
    stats = jnp.sum(stats_ref[...], axis=0)
    lane = iota((1, 128), 1)
    totals = jnp.where(lane < 32, stats, 1.0)
    log_totals = jnp.log(totals)
    terms = jnp.where(
        lane < 32, log_totals + z_weight * log_totals * log_totals, jnp.where(lane < 64, -stats, 0.0)
    )
    loss = jnp.sum(terms, axis=1, keepdims=True) * (1.0 / NQ)
    out_ref[XN * PT :, :] = jnp.broadcast_to(loss, (8, 128))
    slope = 1.0 + 2.0 * z_weight * log_totals
    coefficients = (slope * jnp.exp(logits_ref[...]) / totals - chosen_ref[...]) * (1.0 / NQ)
    factors = by_row(coefficients) * scale_ref[...]
    factors_ref[...] = factors
    total = jnp.zeros((W, ROWS), f32)
    for s in range(XN):
        total = total + ut_a_ref[s] * factors[s : s + 1, :]
        total = total + ut_b_ref[s] * factors[XN + s : XN + s + 1, :]
    dq_ref[...] = total.T
    page_gradients(whi_ref, wlo_ref, qt_ref[...], factors, XN, out_ref)


def own_gradient_kernel(factors_ref, qt_ref, whi_ref, wlo_ref, out_ref):
    page_gradients(whi_ref, wlo_ref, qt_ref[...], factors_ref[...], 0, out_ref)


def pair_kernel(mine_ref, loss_ref, theirs_ref, o0, o1, o2, o3):
    loss = loss_ref[...] + theirs_ref[XN * PT :, :]
    for s, out in enumerate((o0, o1, o2, o3)):
        rows = slice(s * PT, (s + 1) * PT)
        out[0:PT, :] = mine_ref[rows, :] + theirs_ref[rows, :]
        out[PT:, :] = loss


def final_kernel(r0, r1, r2, r3, dq_ref, page_ref, loss_ref, slope_ref):
    total = (r0[...] + r2[...]) + (r1[...] + r3[...])
    page_ref[0] = total[0:PT]
    loss_ref[...] = total[PT : PT + 1, 0:1]
    slope = jnp.zeros((TOK, W), f32)
    for k in range(QN):
        slope = slope + dq_ref[k * TOK : (k + 1) * TOK, :]
    for i in range(TOK):
        slope_ref[i] = slope[i : i + 1, :]


def call(kernel, out, scratch=(), scalars=0, anywhere=0):
    vmem = pl.BlockSpec(memory_space=pltpu.VMEM)

    def run(*args):
        args = [
            pltpu.with_memory_space_constraint(a, pltpu.HBM) if scalars <= i < scalars + anywhere else a
            for i, a in enumerate(args)
        ]
        specs = [pl.BlockSpec(memory_space=pltpu.SMEM)] * scalars
        specs += [pl.BlockSpec(memory_space=pltpu.HBM)] * anywhere
        specs += [vmem] * (len(args) - scalars - anywhere)
        return pl.pallas_call(
            kernel,
            out_shape=[jax.ShapeDtypeStruct(s, d) for s, d in out],
            in_specs=specs,
            out_specs=[vmem] * len(out),
            scratch_shapes=list(scratch),
            compiler_params=pltpu.CompilerParams(vmem_limit_bytes=16 * 1024 * 1024),
        )(*args)

    return run


def moved(value, axis, step):
    bit, mask = axis
    pairs = [
        (i, (i & ~(mask << bit)) | ((((i >> bit) + step) & mask) << bit)) for i in range(DEVICES)
    ]
    return lax.ppermute(value, "d", pairs)


def shards(queries, pages, positive):
    me = lax.axis_index("d").astype(jnp.int32).reshape(1)
    positive = positive.reshape(1, NQ)
    (spread,) = call(
        spread_kernel, [((ROWS, W), f32)],
        [pltpu.VMEM((TOK, 1, W), f32), pltpu.VMEM((2 * TOK, W), f32), pltpu.SemaphoreType.DMA],
        anywhere=1,
    )(queries.transpose(1, 0, 2))
    block = exchange(spread.reshape(QN, TOK, 1, W), QUERY_ORDER).reshape(ROWS, W)
    own = [pages] + [moved(pages, X, s) for s in range(1, XN)]
    other = [moved(page, CO, 1) for page in own]

    weights, terms = ((XN, PT, ROWS), bf16), ((XN, W, ROWS), f32)
    whi_a, wlo_a, ut_a, tot_a, qt, chosen = call(
        own_score_kernel,
        [weights, weights, terms, ((XN, ROWS), f32), ((W, ROWS), f32), ((8, 128), f32)],
        [pltpu.VMEM((1, PT, W), f32), pltpu.VMEM((1, NQ), jnp.int32),
         pltpu.SemaphoreType.DMA, pltpu.SemaphoreType.DMA],
        scalars=1, anywhere=2,
    )(me, pages, positive, block, *own[1:])
    whi_b, wlo_b, ut_b, logits, scale, stats = call(
        score_kernel,
        [weights, weights, terms, ((8, 128), f32), ((2 * XN, ROWS), f32), ((QN, 1, W), f32)],
        [pltpu.VMEM((2 * XN, ROWS), f32)],
    )(qt, tot_a, chosen, *other)
    stats = exchange(stats, STATS_ORDER)
    theirs, factors, dq = call(
        coefficient_kernel, [((XN * PT + 8, W), f32), ((2 * XN, ROWS), f32), ((ROWS, W), f32)]
    )(stats, logits, chosen, scale, qt, whi_b, wlo_b, ut_a, ut_b)
    loss_rows = theirs[XN * PT :]
    theirs = moved(theirs, CO, 1)
    (mine,) = call(own_gradient_kernel, [((XN * PT, W), f32)])(factors, qt, whi_a, wlo_a)
    blocks = call(pair_kernel, [((PT + 8, W), f32)] * XN)(mine, loss_rows, theirs)
    blocks = [blocks[0]] + [moved(blocks[s], X, -s) for s in range(1, XN)]
    dq = exchange(dq.reshape(QN, TOK, 1, W), QUERY_ORDER)
    page_grad, loss, slope = call(
        final_kernel, [((1, PT, W), f32), ((1, 1), f32), ((TOK, 1, W), f32)]
    )(*blocks, dq.reshape(ROWS, W))
    return loss.reshape(()), slope.transpose(1, 0, 2), page_grad


def solution(mesh):
    flat = Mesh(mesh.devices.reshape(DEVICES), ("d",))
    placed = (P("d", None, None), P("d", None, None), P())
    return jax.shard_map(
        shards,
        mesh=flat,
        in_specs=placed,
        out_specs=(P(), P("d", None, None), P("d", None, None)),
        check_vma=False,
    )
```

```python
import jax
import jax.numpy as jnp
from jax import lax
from jax.experimental import pallas as pl
from jax.experimental.pallas import tpu as pltpu
from jax.sharding import Mesh
from jax.sharding import PartitionSpec as P

DEVICES = 256
CO, X = (5, 1), (1, 3)
QN = 32
QUERY_ORDER = (0, 1)
STATS_ORDER = (7, -1)
XN = 4
TOK = 12
ROWS = QN * TOK
PT = 256
W = 128
NQ = 256

cap_value = 4.0
sharpness_divisor = 0.25
logit_scale = 8.0
z_weight = 0.001
f32 = jnp.float32
bf16 = jnp.bfloat16


def offset_of(member):
    return ((member >> 3) << 6) + (((member >> 1) & 3) << 3) + (member & 1)


def groups(order):
    first, step = order
    members = [offset_of((first + step * k) % QN) for k in range(QN)]
    return [[(co << 5) + (x << 1) + m for m in members] for co in range(2) for x in range(XN)]


def exchange(value, order):
    return lax.all_to_all(value, "d", 0, 0, axis_index_groups=groups(order), tiled=True)


def iota(shape, dim):
    return lax.broadcasted_iota(jnp.int32, shape, dim)


def parts(x):
    high = x.astype(bf16)
    return high, (x - high.astype(f32)).astype(bf16)


def product(a, b, dims):
    terms = [
        lax.dot_general(left, right, (dims, ((), ())), preferred_element_type=f32)
        for left, right in ((a[0], b[0]), (a[0], b[1]), (a[1], b[0]))
    ]
    return terms[0] + (terms[1] + terms[2])


def spread_matrix():
    row, lane = iota((ROWS, 128), 0), iota((ROWS, 128), 1)
    first = (lane & 31) * TOK
    return ((row >= first) & (row < first + TOK) & (lane < 64)).astype(f32)


def spread_kernel(q_hbm, out_ref, query_ref, rows_ref, sem):
    copy = pltpu.make_async_copy(q_hbm, query_ref, sem)
    copy.start()
    copy.wait()
    for i in range(TOK):
        rows_ref[i : i + 1, :] = query_ref[i]
        rows_ref[TOK + i : TOK + i + 1, :] = query_ref[i]
    twice = rows_ref[...]
    for k in range(QN // 2):
        out_ref[2 * k * TOK : 2 * (k + 1) * TOK, :] = twice


def is_positive(me_ref, positive_ref):
    me = me_ref[0]
    base = me & 0b00100110
    index, lane = iota((NQ, 128), 0), iota((NQ, 128), 1)
    query = offset_of((QUERY_ORDER[0] + QUERY_ORDER[1] * lane) & (QN - 1)) + base
    chosen = jnp.dot(
        positive_ref[...].astype(f32), (index == query).astype(f32), precision=lax.Precision.HIGHEST,
        preferred_element_type=f32,
    )
    row = iota((8, 128), 0)
    x = (((me >> 1) & 3) - (row & 3)) & 3
    co = ((me >> 5) & 1) ^ (row >> 2)
    page = (me & 0b11011001) + (x << 1) + (co << 5)
    return page.astype(f32) == chosen


def by_row(values):
    return lax.dot_general(
        jnp.where(iota((8, 128), 1) < 32, values, 0.0), spread_matrix(), (((1,), (1,)), ((), ())),
        precision=lax.Precision.HIGHEST, preferred_element_type=f32,
    )


def page_terms(q_parts, page, s, whi_ref, wlo_ref, tot_ref):
    scores = product(parts(page), q_parts, ((1,), (0,)))
    tangent = jnp.tanh(scores * (1.0 / cap_value))
    grid = jnp.exp(tangent * (cap_value / sharpness_divisor))
    tot_ref[s : s + 1, :] = jnp.sum(grid, axis=0, keepdims=True)
    whi_ref[s], wlo_ref[s] = parts(grid * (1.0 - tangent * tangent))


def query_terms(page, s, whi_ref, wlo_ref, ut_ref):
    ut_ref[s] = product(parts(page.T), (whi_ref[s], wlo_ref[s]), ((1,), (0,)))


def own_score_kernel(
    me_ref, own_hbm, positive_hbm, q_ref, p1, p2, p3,
    whi_ref, wlo_ref, ut_ref, tot_ref, qt_ref, chosen_ref, p0, positive_ref, own_sem, positive_sem,
):
    own_copy = pltpu.make_async_copy(own_hbm, p0, own_sem)
    positive_copy = pltpu.make_async_copy(positive_hbm, positive_ref, positive_sem)
    own_copy.start()
    positive_copy.start()
    qt = q_ref[...].T
    qt_ref[...] = qt
    q_parts = parts(qt)
    pages = (p0, p1, p2, p3)
    for s in range(1, XN):
        page_terms(q_parts, pages[s][0], s, whi_ref, wlo_ref, tot_ref)
    own_copy.wait()
    page_terms(q_parts, p0[0], 0, whi_ref, wlo_ref, tot_ref)
    for s in range(XN):
        query_terms(pages[s][0], s, whi_ref, wlo_ref, ut_ref)
    positive_copy.wait()
    chosen_ref[...] = is_positive(me_ref, positive_ref).astype(f32)


def score_kernel(
    qt_ref, tot_a_ref, chosen_ref, p0, p1, p2, p3,
    whi_ref, wlo_ref, ut_ref, logits_ref, scale_ref, stats_ref, tot_ref,
):
    tot_ref[0:XN, :] = tot_a_ref[...]
    q_parts = parts(qt_ref[...])
    pages = (p0, p1, p2, p3)
    for s in range(XN):
        page_terms(q_parts, pages[s][0], s, whi_ref, wlo_ref, tot_ref.at[XN : 2 * XN])
    smooth = sharpness_divisor * jnp.log(tot_ref[...])
    logits = (logit_scale / TOK) * jnp.dot(
        smooth, spread_matrix(), precision=lax.Precision.HIGHEST, preferred_element_type=f32
    )
    logits_ref[...] = logits
    scale_ref[...] = (logit_scale / TOK) / tot_ref[...]
    lane = iota((8, 128), 1)
    matched = jnp.where(chosen_ref[...] > 0.5, logits, 0.0)
    local = jnp.where(lane < 32, jnp.exp(logits), jnp.where(lane < 64, matched, 0.0))
    stats = jnp.sum(local, axis=0, keepdims=True)
    stats_ref[...] = jnp.broadcast_to(stats[None], stats_ref.shape)
    for s in range(XN):
        query_terms(pages[s][0], s, whi_ref, wlo_ref, ut_ref)


def page_gradients(whi_ref, wlo_ref, qt, factors, first, out_ref):
    for s in range(XN):
        scaled = parts(qt * factors[first + s : first + s + 1, :])
        out_ref[s * PT : (s + 1) * PT, :] = product(
            (whi_ref[s], wlo_ref[s]), scaled, ((1,), (1,))
        )


def coefficient_kernel(
    stats_ref, logits_ref, chosen_ref, scale_ref, qt_ref, whi_ref, wlo_ref, ut_a_ref, ut_b_ref,
    out_ref, factors_ref, dq_ref,
):
    stats = jnp.sum(stats_ref[...], axis=0)
    lane = iota((1, 128), 1)
    totals = jnp.where(lane < 32, stats, 1.0)
    log_totals = jnp.log(totals)
    terms = jnp.where(
        lane < 32, log_totals + z_weight * log_totals * log_totals, jnp.where(lane < 64, -stats, 0.0)
    )
    loss = jnp.sum(terms, axis=1, keepdims=True) * (1.0 / NQ)
    out_ref[XN * PT :, :] = jnp.broadcast_to(loss, (8, 128))
    slope = 1.0 + 2.0 * z_weight * log_totals
    coefficients = (slope * jnp.exp(logits_ref[...]) / totals - chosen_ref[...]) * (1.0 / NQ)
    factors = by_row(coefficients) * scale_ref[...]
    factors_ref[...] = factors
    total = jnp.zeros((W, ROWS), f32)
    for s in range(XN):
        total = total + ut_a_ref[s] * factors[s : s + 1, :]
        total = total + ut_b_ref[s] * factors[XN + s : XN + s + 1, :]
    dq_ref[...] = total.T
    page_gradients(whi_ref, wlo_ref, qt_ref[...], factors, XN, out_ref)


def own_gradient_kernel(factors_ref, qt_ref, whi_ref, wlo_ref, out_ref):
    page_gradients(whi_ref, wlo_ref, qt_ref[...], factors_ref[...], 0, out_ref)


def pair_kernel(mine_ref, loss_ref, theirs_ref, o0, o1, o2, o3):
    loss = loss_ref[...] + theirs_ref[XN * PT :, :]
    for s, out in enumerate((o0, o1, o2, o3)):
        rows = slice(s * PT, (s + 1) * PT)
        out[0:PT, :] = mine_ref[rows, :] + theirs_ref[rows, :]
        out[PT:, :] = loss


def final_kernel(r0, r1, r2, r3, dq_ref, page_ref, loss_ref, slope_ref):
    total = (r0[...] + r2[...]) + (r1[...] + r3[...])
    page_ref[0] = total[0:PT]
    loss_ref[...] = total[PT : PT + 1, 0:1]
    slope = jnp.zeros((TOK, W), f32)
    for k in range(QN):
        slope = slope + dq_ref[k * TOK : (k + 1) * TOK, :]
    for i in range(TOK):
        slope_ref[i] = slope[i : i + 1, :]


def call(kernel, out, scratch=(), scalars=0, anywhere=0):
    vmem = pl.BlockSpec(memory_space=pltpu.VMEM)

    def run(*args):
        args = [
            pltpu.with_memory_space_constraint(a, pltpu.HBM) if scalars <= i < scalars + anywhere else a
            for i, a in enumerate(args)
        ]
        specs = [pl.BlockSpec(memory_space=pltpu.SMEM)] * scalars
        specs += [pl.BlockSpec(memory_space=pltpu.HBM)] * anywhere
        specs += [vmem] * (len(args) - scalars - anywhere)
        return pl.pallas_call(
            kernel,
            out_shape=[jax.ShapeDtypeStruct(s, d) for s, d in out],
            in_specs=specs,
            out_specs=[vmem] * len(out),
            scratch_shapes=list(scratch),
            compiler_params=pltpu.CompilerParams(vmem_limit_bytes=16 * 1024 * 1024),
        )(*args)

    return run


def moved(value, axis, step):
    bit, mask = axis
    pairs = [
        (i, (i & ~(mask << bit)) | ((((i >> bit) + step) & mask) << bit)) for i in range(DEVICES)
    ]
    return lax.ppermute(value, "d", pairs)


def shards(queries, pages, positive):
    me = lax.axis_index("d").astype(jnp.int32).reshape(1)
    positive = positive.reshape(1, NQ)
    (spread,) = call(
        spread_kernel, [((ROWS, W), f32)],
        [pltpu.VMEM((TOK, 1, W), f32), pltpu.VMEM((2 * TOK, W), f32), pltpu.SemaphoreType.DMA],
        anywhere=1,
    )(queries.transpose(1, 0, 2))
    block = exchange(spread.reshape(QN, TOK, 1, W), QUERY_ORDER).reshape(ROWS, W)
    passed = {s: moved(pages, X, s) for s in (1, 3, 2)}
    own = [pages] + [passed[s] for s in range(1, XN)]
    other = [moved(page, CO, 1) for page in own]

    weights, terms = ((XN, PT, ROWS), bf16), ((XN, W, ROWS), f32)
    whi_a, wlo_a, ut_a, tot_a, qt, chosen = call(
        own_score_kernel,
        [weights, weights, terms, ((XN, ROWS), f32), ((W, ROWS), f32), ((8, 128), f32)],
        [pltpu.VMEM((1, PT, W), f32), pltpu.VMEM((1, NQ), jnp.int32),
         pltpu.SemaphoreType.DMA, pltpu.SemaphoreType.DMA],
        scalars=1, anywhere=2,
    )(me, pages, positive, block, *own[1:])
    whi_b, wlo_b, ut_b, logits, scale, stats = call(
        score_kernel,
        [weights, weights, terms, ((8, 128), f32), ((2 * XN, ROWS), f32), ((QN, 1, W), f32)],
        [pltpu.VMEM((2 * XN, ROWS), f32)],
    )(qt, tot_a, chosen, *other)
    stats = exchange(stats, STATS_ORDER)
    theirs, factors, dq = call(
        coefficient_kernel, [((XN * PT + 8, W), f32), ((2 * XN, ROWS), f32), ((ROWS, W), f32)]
    )(stats, logits, chosen, scale, qt, whi_b, wlo_b, ut_a, ut_b)
    loss_rows = theirs[XN * PT :]
    theirs = moved(theirs, CO, 1)
    (mine,) = call(own_gradient_kernel, [((XN * PT, W), f32)])(factors, qt, whi_a, wlo_a)
    blocks = call(pair_kernel, [((PT + 8, W), f32)] * XN)(mine, loss_rows, theirs)
    returned = {s: moved(blocks[s], X, -s) for s in (2, 1, 3)}
    blocks = [blocks[0]] + [returned[s] for s in range(1, XN)]
    dq = exchange(dq.reshape(QN, TOK, 1, W), QUERY_ORDER)
    page_grad, loss, slope = call(
        final_kernel, [((1, PT, W), f32), ((1, 1), f32), ((TOK, 1, W), f32)]
    )(*blocks, dq.reshape(ROWS, W))
    return loss.reshape(()), slope.transpose(1, 0, 2), page_grad


def solution(mesh):
    flat = Mesh(mesh.devices.reshape(DEVICES), ("d",))
    placed = (P("d", None, None), P("d", None, None), P())
    return jax.shard_map(
        shards,
        mesh=flat,
        in_specs=placed,
        out_specs=(P(), P("d", None, None), P("d", None, None)),
        check_vma=False,
    )
```
